256 devices in a mesh: freq: 32 (over y, z), pencil: 8 (over x, core).
Axes of the slice: x: 4, y: 4, z: 8, core: 2. Of those that a mesh axis runs over, the one named last changes fastest.
Arguments:
- wave_field: float32 [64, 512, 2, 512], P('freq', 'pencil'), may hold values from -6 to 6
- source_field: float32 [1, 64, 512, 2, 512], P(None, 'freq', 'pencil'), may hold values from -6 to 6
- omegas: float32 [64], P('freq'), may hold values from 30 to 250
- velocities: float32 [1, 6], replicated, may hold values from 1500 to 4500
- lower_ref: int32 [1, 8, 8], replicated, may hold values from 0 to 4, as said below
- blend_weight: float32 [1, 8, 8], replicated, may hold values from 0 to 1
Outputs:
- new_field: float32 [64, 512, 2, 512], P('freq', 'pencil')
- image: float32 [1, 512, 512], P(None, 'pencil', 'freq')
The draws below stay inside these ranges and needn't reach their ends.
Inputs may be any that keep to these rules, and one draw needn't show every extreme that they name: `lower_ref`: in each depth step the lower references of one tile row differ by at most one, so a tile row's tiles use at most three consecutive references; in each depth step one tile row uses references 0 to 2 and another references 6 - 3 to 5.
All inputs are finite; a program needn't handle non-finite values.
Results may differ from the reference program's by a relative error of at most 0.0001.
Values sent between devices are 32-bit elements; how exact they have to be, the bound alone decides.
No kernel may reach another device: no remote copies, remote signals or barrier semaphores. Data moves between devices by JAX's collectives and lax.ppermute only.
A program may use at most 128 MiB of HBM per device.

```python
import math
import jax
import jax.numpy as jnp
from jax import lax

NX = 512
NY = 512
TILE = 64
NREF = 6
DEPTHS = 1
NW = 64
NTX = 8
NTY = 8


def draw_lower_ref(key, part):

    def one_depth(depth_key):
        key_base, key_step, key_rows = jax.random.split(depth_key, 3)
        rows_count = NX // TILE
        cols_count = NY // TILE
        base_row = jax.random.randint(key_base, (rows_count, 1), 0, NREF - 2)
        step_tile = jax.random.randint(key_step, (rows_count, cols_count), 0, 2)
        order = jax.random.permutation(key_rows, rows_count)
        row_ids = jnp.arange(rows_count)[:, None]
        col_ids = jnp.arange(cols_count)[None, :]
        base_row = jnp.where(row_ids == order[0], 0, base_row)
        base_row = jnp.where(row_ids == order[1], NREF - 3, base_row)
        forced = (row_ids == order[0]) | (row_ids == order[1])
        step_tile = jnp.where(forced & (col_ids == 0), 0, step_tile)
        step_tile = jnp.where(forced & (col_ids == 1), 1, step_tile)
        return (base_row + step_tile).astype(jnp.int32)
    return jax.vmap(one_depth)(jax.random.split(jax.random.fold_in(key, 17), DEPTHS))


def raised(array, rng, source, target, shards_of, factor):
    owner, partner = [(jnp.arange(array.shape[dim]) // (array.shape[dim] // shards_of)).reshape([-1 if axis == dim else 1 for axis in range(array.ndim)]) for dim in (source, target)]
    chosen = jax.random.permutation(rng, shards_of)[partner]
    strong = (owner == chosen) | (owner == (partner + shards_of // 2) % shards_of)
    return jnp.where(strong, factor * array, array)


def levels(rng, dims, cuts, smallest, top_value):
    loudness = 1.0
    for position, shards_of in cuts:
        steps = jax.random.uniform(jax.random.fold_in(jax.random.fold_in(rng, 6), position), (shards_of,), jnp.float32, smallest / len(cuts), top_value / len(cuts))
        loudness = loudness * jnp.repeat(jnp.exp(steps), dims[position] // shards_of).reshape((-1,) + (1,) * (len(dims) - 1 - position))
    return loudness


def noise(own_key, dims, spread, reach, cuts=(), kind=jnp.bfloat16):
    drawn = spread * jax.random.normal(own_key, dims, jnp.float32)
    if cuts:
        drawn = drawn * levels(own_key, dims, cuts, -0.22, 0.18)
    return jnp.clip(drawn, -reach, reach).astype(kind)


def gaussian_with(stream_key, extent, deviation, limit, cuts, heavy, kind=jnp.bfloat16):
    array = deviation * jax.random.normal(stream_key, extent, jnp.float32)
    if cuts:
        array = array * levels(stream_key, extent, cuts, -0.22, 0.18)
    return jnp.clip(raised(array, jax.random.fold_in(stream_key, 3), *heavy), -limit, limit).astype(kind)


def setup_inputs(seed: int = 0) -> dict:
    splits = jax.random.split(jax.random.key(seed), 7)
    wave_field = noise(splits[0], (NW, NX, 2, NY), 1.0, 6.0, ((0, 32), (1, 8)), jnp.float32)
    source_field = gaussian_with(splits[1], (DEPTHS, NW, NX, 2, NY), 1.0, 6.0, ((1, 32), (2, 8)), (1, 4, 32, 2.75), jnp.float32)
    omegas = jnp.clip(30.0 + 220.0 * jax.random.uniform(splits[2], (NW,), jnp.float32) ** levels(splits[2], (NW,), ((0, 32),), -0.2, 0.2), 30.0, 250.0)
    velocities = jnp.clip(jax.random.uniform(splits[3], (DEPTHS, NREF), jnp.float32, 1500.0, 4500.0), 1500.0, 4500.0)
    lower_ref = draw_lower_ref(jax.random.fold_in(splits[6], 71), 0)
    blend_weight = jnp.clip(jax.random.uniform(splits[5], (DEPTHS, NTX, NTY), jnp.float32, 0.0, 1.0), 0.0, 1.0)
    return {"wave_field": wave_field, "source_field": source_field, "omegas": omegas, "velocities": velocities, "lower_ref": lower_ref, "blend_weight": blend_weight}


GRID_SPACING = 12.5
DEPTH_STEP = 10.0

def wave_numbers(amount, offset, length):
    index_all = offset + jnp.arange(amount, dtype=jnp.int32)
    signed = jnp.where(index_all < length // 2, index_all, index_all - length)
    return signed.astype(jnp.float32) * (2.0 * math.pi / (length * GRID_SPACING))

def phase_terms(angular, velocity, radial):
    vertical = (angular / velocity) ** 2 - radial
    travel = jnp.sqrt(jnp.maximum(vertical, 0.0)) * DEPTH_STEP
    damping = jnp.exp(-jnp.sqrt(jnp.maximum(-vertical, 0.0)) * DEPTH_STEP)
    return (damping * jnp.cos(travel), damping * jnp.sin(travel))

def tile_coefficients(lower_idx, weight, ref_value):
    return jnp.where(lower_idx == ref_value, weight, 0.0) + jnp.where(lower_idx + 1 == ref_value, 1.0 - weight, 0.0)

def reference(wave_field, source_field, omegas, velocities, lower_ref, blend_weight):
    radial = wave_numbers(NX, 0, NX)[:, None] ** 2 + wave_numbers(NY, 0, NY)[None, :] ** 2
    wavefield = wave_field
    images = []
    image_scale = 1.0 / math.sqrt(NW)
    for depth_index in range(DEPTHS):
        lower_pix = jnp.repeat(jnp.repeat(lower_ref[depth_index], TILE, axis=0), TILE, axis=1)
        weight_pix = jnp.repeat(jnp.repeat(blend_weight[depth_index], TILE, axis=0), TILE, axis=1)
        coefficients = [tile_coefficients(lower_pix, weight_pix, ref_index) for ref_index in range(NREF)]
        speeds = velocities[depth_index]

        def extrapolate(element):
            frequency_plane, angular = element
            spectrum = jnp.fft.fft2(frequency_plane[:, 0] + 1j * frequency_plane[:, 1], norm='ortho')
            total_real = jnp.zeros((NX, NY), jnp.float32)
            total_imag = jnp.zeros((NX, NY), jnp.float32)
            for ref_index in range(NREF):
                cos_part, sin_part = phase_terms(angular, speeds[ref_index], radial)
                shifted = jnp.fft.ifft2(spectrum * (cos_part + 1j * sin_part), norm='ortho')
                total_real = total_real + coefficients[ref_index] * jnp.real(shifted)
                total_imag = total_imag + coefficients[ref_index] * jnp.imag(shifted)
            return jnp.stack([total_real, total_imag], axis=1)
        wavefield = lax.map(extrapolate, (wavefield, omegas))
        source = source_field[depth_index]
        depth_image = lax.optimization_barrier(jnp.sum(source[:, :, 0] * wavefield[:, :, 0] + source[:, :, 1] * wavefield[:, :, 1], axis=0)) * image_scale
        images.append(depth_image)
    return (wavefield, jnp.stack(images))
```

```python
import math

import jax
import jax.numpy as jnp
import numpy as np
from jax import lax
from jax.experimental import pallas as pl
from jax.experimental.pallas import tpu as pltpu
from jax.sharding import PartitionSpec as P


N = 512
TILE = 64
NREF = 6
NEED = 3
STEP = 10.0
UNIT = 2.0 * math.pi / (N * 12.5)
HALF = N // 2
BF = jnp.bfloat16
F32 = jnp.float32
INTERPRET = False


def split(values):
    high = values.astype(BF)
    return high, (values - high.astype(F32)).astype(BF)


def hartley():
    turn = (np.arange(N)[:, None] * np.arange(N)[None, :] % N) * (2.0 * np.pi / N)
    return (np.cos(turn) + np.sin(turn)) / np.sqrt(N)


def tables():
    plain = hartley()
    order = np.concatenate([np.arange(HALF), [HALF], N - np.arange(1, HALF)])
    folded = plain[order]
    out = []
    for table in (plain, folded, folded.T):
        high = np.asarray(table, np.float32).astype(jnp.bfloat16)
        low = (table - high.astype(np.float64)).astype(np.float32).astype(jnp.bfloat16)
        out += [high, low]
    return out


def dot3(left, right):
    lh, ll = left
    rh, rl = right
    d = lambda a, b: jnp.dot(a, b, preferred_element_type=F32)
    return d(lh, rh) + (d(lh, rl) + d(ll, rh))


def low_lanes(shape):
    return lax.broadcasted_iota(jnp.int32, shape, len(shape) - 1) < 64


def forward_y(wave_ref, high_ref, low_ref, out_ref):
    table = (high_ref[...], low_ref[...])
    for f in range(2):
        real = dot3(split(wave_ref[f, 0]), table)
        imag = dot3(split(wave_ref[f, 1]), table)
        first = low_lanes((64, 128))
        for m in range(4):
            re = real[:, 128 * m : 128 * m + 128]
            im = imag[:, 128 * m : 128 * m + 128]
            out_ref[2 * m, f] = jnp.where(first, re, pltpu.roll(im, 64, 1))
            out_ref[2 * m + 1, f] = jnp.where(first, pltpu.roll(re, 64, 1), im)


def phase_of(q):
    root = jnp.sqrt(jnp.abs(q)) * STEP
    u = jnp.maximum(q, 0.0) * (STEP * STEP)
    cosine = jnp.full_like(u, 1.0 / math.factorial(16))
    for k in range(7, -1, -1):
        cosine = cosine * u + (-1.0) ** k / math.factorial(2 * k)
    sine = jnp.full_like(u, -1.0 / math.factorial(15))
    for k in range(6, -1, -1):
        sine = sine * u + (-1.0) ** k / math.factorial(2 * k + 1)
    damping = jnp.exp(-root)
    moving = q > 0.0
    return jnp.where(moving, cosine, damping), jnp.where(moving, sine * root, 0.0)


def phases(pos_ref, omega_ref, speed_ref, cos_ref, sin_ref, nyq_ref):
    lane = lax.broadcasted_iota(jnp.int32, (128, 128), 1)
    row = lax.broadcasted_iota(jnp.int32, (128, 128), 0)
    ky = pos_ref[0] * 64 + (lane & 63)
    ky = jnp.where(ky < HALF, ky, ky - N).astype(F32) * UNIT
    kx = (row + 2 * (lane & 64)).astype(F32) * UNIT
    ky2 = ky * ky
    radial = kx * kx + ky2
    edge = (HALF * UNIT) ** 2 + ky2[:8]
    for f in range(2):
        for r in range(NREF):
            ratio = omega_ref[f] / speed_ref[r]
            square = ratio * ratio
            c, s = phase_of(square - radial)
            cos_ref[f, r] = c
            sin_ref[f, r] = s
            c, s = phase_of(square - edge)
            nyq_ref[f, r, 0] = c
            nyq_ref[f, r, 1] = s


def shift_x(base_ref, came_ref, cos_ref, sin_ref, nyq_ref, ah_ref, al_ref, bh_ref, bl_ref, out_ref, spec, swapped, th, tl):
    wave = jnp.concatenate([came_ref[:, f].reshape(N, 128) for f in range(2)], axis=1)
    found = dot3((ah_ref[...], al_ref[...]), split(wave))
    spec[...] = found
    swapped[...] = jnp.concatenate([pltpu.roll(found[:, 128 * f : 128 * f + 128], 64, 1) for f in range(2)], axis=1)
    first = low_lanes((128, 128))
    first8 = low_lanes((8, 128))
    top = lax.broadcasted_iota(jnp.int32, (8, 128), 0) == 0
    for r in range(NREF):
        for f in range(2):
            lanes = pl.ds(128 * f, 128)
            c = cos_ref[f, r]
            s = sin_ref[f, r]
            cr = pltpu.roll(c, 64, 1)
            sr = pltpu.roll(s, 64, 1)
            parts = (
                (jnp.where(first, c, cr), jnp.where(first, -s, sr)),
                (jnp.where(first, cr, c), jnp.where(first, -sr, s)),
            )
            for half in range(2):
                for part in range(2):
                    cc, ss = parts[part]
                    start = 256 * half + 128 * part
                    if half == 1 and part == 0:
                        nc = nyq_ref[f, r, 0]
                        ns = nyq_ref[f, r, 1]
                        ns = jnp.where(first8, -ns, ns)
                        cc = jnp.concatenate([jnp.where(top, nc, cc[:8]), cc[8:]], axis=0)
                        ss = jnp.concatenate([jnp.where(top, ns, ss[:8]), ss[8:]], axis=0)
                    rows = pl.ds(start, 128)
                    moved = spec[rows, lanes] * cc + swapped[rows, lanes] * ss
                    high, low = split(moved)
                    th[r % 2, rows, lanes] = high
                    tl[r % 2, rows, lanes] = low
        back = dot3((bh_ref[...], bl_ref[...]), (th[r % 2], tl[r % 2]))
        for p in range(8):
            j = r - base_ref[p]

            @pl.when((j >= 0) & (j < NEED))
            def _(p=p, j=j, back=back):
                for f in range(2):
                    out_ref[p, j, f] = back[64 * p : 64 * p + 64, 128 * f : 128 * f + 128]


def inverse_y(coef_ref, came_ref, source_ref, high_ref, low_ref, out_ref, image_ref):
    table = (high_ref[...], low_ref[...])
    first = low_lanes((64, 128))
    image = None
    for f in range(2):
        fields = [None, None]
        for j in range(NEED):
            re, im = [], []
            for m in range(4):
                a = came_ref[2 * m, j, f]
                b = came_ref[2 * m + 1, j, f]
                re.append(jnp.where(first, a, pltpu.roll(b, 64, 1)))
                im.append(jnp.where(first, pltpu.roll(a, 64, 1), b))
            coef = coef_ref[j : j + 1, :]
            for c, pieces in enumerate((re, im)):
                space = dot3(split(jnp.concatenate(pieces, axis=1)), table) * coef
                fields[c] = space if j == 0 else fields[c] + space
        for c in range(2):
            out_ref[f, c] = fields[c]
            term = fields[c] * source_ref[f, c]
            image = term if image is None else image + term
    image = image * (1.0 / 8.0)
    group = lax.broadcasted_iota(jnp.int32, (8, 128), 1) // 16
    for t in range(4):
        cells = [image[8 * b : 8 * b + 8, 128 * t : 128 * t + 128] for b in range(8)]
        for bit in (1, 2, 4):
            low = (group & bit) == 0
            new = [None] * 8
            for b in range(8):
                if b & bit:
                    continue
                x, y = cells[b], cells[b | bit]
                new[b] = jnp.where(low, x, pltpu.roll(y, 16 * bit, 1))
                new[b | bit] = jnp.where(low, pltpu.roll(x, 128 - 16 * bit, 1), y)
            cells = new
        for g in range(8):
            image_ref[8 * t + g] = cells[g]


def sum_image(came_ref, out_ref):
    total = jnp.sum(came_ref[...], axis=0)
    for b in range(8):
        out_ref[0, 8 * b : 8 * b + 8, :] = total[:, 16 * b : 16 * b + 16]


VM = pl.BlockSpec(memory_space=pltpu.VMEM)
SM = pl.BlockSpec(memory_space=pltpu.SMEM)


def call(body, out, specs, scratch=()):
    many = isinstance(out, (tuple, list))
    return pl.pallas_call(
        body,
        out_shape=out,
        in_specs=specs,
        out_specs=tuple(VM for _ in out) if many else VM,
        scratch_shapes=list(scratch),
        compiler_params=pltpu.CompilerParams(vmem_limit_bytes=56 * 2**20),
        interpret=INTERPRET,
        name=body.__name__,
    )


def shape(*dims):
    return jax.ShapeDtypeStruct(dims, F32)


def on_device(wave_field, source_field, omegas, velocities, lower_ref, blend_weight):
    position = lax.axis_index("pencil")
    yh, yl, ah, al, bh, bl = (jnp.asarray(t) for t in tables())
    base = jnp.minimum(jnp.min(lower_ref[0], axis=1), NREF - NEED)
    lower = lax.dynamic_index_in_dim(lower_ref[0], position, 0, False)
    weight = lax.dynamic_index_in_dim(blend_weight[0], position, 0, False)
    offset = lower - lax.dynamic_index_in_dim(base, position, 0, False)
    index = jnp.arange(NEED)[:, None]
    coef = jnp.where(offset == index, weight, 0.0) + jnp.where(offset + 1 == index, 1.0 - weight, 0.0)
    coef = jnp.repeat(coef, TILE, axis=1)

    wave = jnp.transpose(wave_field, (0, 2, 1, 3))
    sent = call(forward_y, shape(8, 2, 64, 128), [VM] * 3)(wave, yh, yl)
    came = lax.all_to_all(sent.reshape(8, 128, 128), "pencil", 0, 0, tiled=True).reshape(8, 2, 64, 128)
    cosine, sine, nyquist = call(
        phases, (shape(2, NREF, 128, 128), shape(2, NREF, 128, 128), shape(2, NREF, 2, 8, 128)), [SM] * 3
    )(position.reshape(1), omegas, velocities[0])
    sent = call(
        shift_x,
        shape(8, NEED, 2, 64, 128),
        [SM] + [VM] * 8,
        [pltpu.VMEM((N, 256), F32)] * 2 + [pltpu.VMEM((2, N, 256), BF)] * 2,
    )(base, came, cosine, sine, nyquist, ah, al, bh, bl)
    came = lax.all_to_all(sent.reshape(8, 384, 128), "pencil", 0, 0, tiled=True).reshape(8, NEED, 2, 64, 128)
    source = jnp.transpose(source_field[0], (0, 2, 1, 3))
    field, image = call(inverse_y, (shape(2, 2, 64, N), shape(32, 8, 128)), [VM] * 5)(coef, came, source, yh, yl)
    return finish(field, image)


def finish(field, image):
    came = lax.all_to_all(image, "freq", 0, 0, tiled=True)
    image = call(sum_image, shape(1, 64, 16), [VM])(came)
    return jnp.transpose(field, (0, 2, 1, 3)), image


def solution(mesh):
    placed = (
        P("freq", "pencil", None, None),
        P(None, "freq", "pencil", None, None),
        P("freq"),
        P(),
        P(),
        P(),
    )
    return jax.shard_map(
        on_device,
        mesh=mesh,
        in_specs=placed,
        out_specs=(P("freq", "pencil", None, None), P(None, "pencil", "freq")),
        check_vma=False,
    )
```

```python
import functools
import math

import jax
import jax.numpy as jnp
import numpy as np
from jax import lax
from jax.experimental import pallas as pl
from jax.experimental.pallas import tpu as pltpu
from jax.sharding import PartitionSpec as P


N = 512
NREF = 6
NEED = 3
STEP = 10.0
UNIT = 2.0 * math.pi / (N * 12.5)
HALF = N // 2
QUART = N // 4
SLOTS = ((2, 0), (2, 1), (1, 0), (1, 1), (3, 0), (3, 1), (0, 1), (0, 0))
BF = jnp.bfloat16
F32 = jnp.float32
INTERPRET = False


def split(values):
    high = values.astype(BF)
    return high, (values - high.astype(F32)).astype(BF)


def tables():
    place = np.arange(HALF)
    cas = lambda k: (lambda t: np.cos(t) + np.sin(t))((place[:, None] * k[None, :] % N) * (2.0 * np.pi / N)) / np.sqrt(N)
    even, odd = cas(2 * place), cas(2 * place + 1)
    j = np.arange(QUART)
    fold_even = cas(np.concatenate([2 * j, [HALF], N - 2 * j[1:]]))
    fold_odd = cas(np.concatenate([2 * j + 1, N - 1 - 2 * j]))
    out = []
    for table in (even, odd, odd.T, fold_even.T, fold_odd.T, fold_even, fold_odd):
        high = np.asarray(table, np.float32).astype(jnp.bfloat16)
        low = (table - high.astype(np.float64)).astype(np.float32).astype(jnp.bfloat16)
        out.append(np.stack([high, low]))
    return out


def cat_left(pair):
    high, low = pair
    return jnp.concatenate([high, high, low], axis=1)


def cat_right(pair):
    high, low = pair
    return jnp.concatenate([high, low, high], axis=0)


def dot3(left, right):
    return jnp.dot(cat_left(left), cat_right(right), preferred_element_type=F32)


def both(ref):
    return ref[0], ref[1]


def low_lanes(shape):
    return lax.broadcasted_iota(jnp.int32, shape, len(shape) - 1) < 64


def forward_y(wave_ref, even_ref, odd_ref, out_ref):
    rows = jnp.concatenate([wave_ref[f, :, c, :] for f in range(2) for c in range(2)], axis=0)
    near, far = rows[:, :HALF], rows[:, HALF:]
    first = low_lanes((64, 128))
    for kind, (mixed, ref) in enumerate(((near + far, even_ref), (near - far, odd_ref))):
        spectrum = dot3(split(mixed), both(ref))
        for f in range(2):
            for m in range(2):
                lanes = slice(128 * m, 128 * m + 128)
                re = spectrum[128 * f : 128 * f + 64, lanes]
                im = spectrum[128 * f + 64 : 128 * f + 128, lanes]
                out_ref[4 * kind + 2 * m, f] = jnp.where(first, re, pltpu.roll(im, 64, 1))
                out_ref[4 * kind + 2 * m + 1, f] = jnp.where(first, pltpu.roll(re, 64, 1), im)


def phase_of(q):
    root = jnp.sqrt(jnp.abs(q)) * STEP
    u = jnp.maximum(q, 0.0) * (STEP * STEP)
    cosine = jnp.full_like(u, 1.0 / math.factorial(16))
    for k in range(7, -1, -1):
        cosine = cosine * u + (-1.0) ** k / math.factorial(2 * k)
    sine = jnp.full_like(u, -1.0 / math.factorial(15))
    for k in range(6, -1, -1):
        sine = sine * u + (-1.0) ** k / math.factorial(2 * k + 1)
    damping = jnp.exp(-root)
    moving = q > 0.0
    return jnp.where(moving, cosine, damping), jnp.where(moving, sine * root, 0.0)


def phases(pos_ref, omega_ref, speed_ref, cos_ref, sin_ref, nyq_ref):
    lane = lax.broadcasted_iota(jnp.int32, (QUART, 128), 1)
    row = lax.broadcasted_iota(jnp.int32, (QUART, 128), 0)
    pos = pos_ref[0]
    ky = 2 * (64 * (pos % 4) + (lane & 63)) + pos // 4
    ky = jnp.where(ky < HALF, ky, ky - N).astype(F32) * UNIT
    kx = (2 * row + lane // 64).astype(F32) * UNIT
    ky2 = ky * ky
    radial = kx * kx + ky2
    edge = (HALF * UNIT) ** 2 + ky2[:8]
    for f in range(2):
        for r in range(NREF):
            ratio = omega_ref[f] / speed_ref[r]
            square = ratio * ratio
            c, s = phase_of(square - radial)
            cos_ref[f, r] = c
            sin_ref[f, r] = s
            c, s = phase_of(square - edge)
            nyq_ref[f, r, 0] = c
            nyq_ref[f, r, 1] = s


def dest_of(pos, slot):
    chips, core = SLOTS[slot]
    return ((pos // 2 + chips) % 4) * 2 + (pos % 2 + core) % 2


def source_of(pos, slot):
    chips, core = SLOTS[slot]
    return ((pos // 2 + 4 - chips) % 4) * 2 + (pos % 2 + core) % 2


def shift_x(f, pos_ref, lower_ref, came_ref, cos_ref, sin_ref, nyq_ref, ae_ref, ao_ref, be_ref, bo_ref, *refs):
    outs, (spec, swapped, back) = refs[:8], refs[8:]
    near = came_ref[0:4, f].reshape(HALF, 128)
    far = came_ref[4:8, f].reshape(HALF, 128)
    for kind, (mixed, ref) in enumerate(((near + far, ae_ref), (near - far, ao_ref))):
        found = dot3(both(ref), split(mixed))
        spec[kind] = found
        swapped[kind] = pltpu.roll(found, 64, 1)
    first = low_lanes((QUART, 128))
    first8 = low_lanes((8, 128))
    top = lax.broadcasted_iota(jnp.int32, (8, 128), 0) == 0
    inverse = (cat_left(both(be_ref)), cat_left(both(bo_ref)))
    for pair in range(NREF // 2):
        moved = [[], []]
        for r in (2 * pair, 2 * pair + 1):
            c = cos_ref[f, r]
            s = sin_ref[f, r]
            cr = pltpu.roll(c, 64, 1)
            sr = pltpu.roll(s, 64, 1)
            parts = (
                (jnp.where(first, c, cr), jnp.where(first, -s, sr)),
                (jnp.where(first, cr, c), jnp.where(first, -sr, s)),
            )
            nc = nyq_ref[f, r, 0]
            ns = nyq_ref[f, r, 1]
            ns = jnp.where(first8, -ns, ns)
            for kind in range(2):
                blocks = []
                for block in range(2):
                    cc, ss = parts[kind]
                    if kind == 0 and block == 1:
                        cc = jnp.concatenate([jnp.where(top, nc, cc[:8]), cc[8:]], axis=0)
                        ss = jnp.concatenate([jnp.where(top, ns, ss[:8]), ss[8:]], axis=0)
                    rows = pl.ds(QUART * block, QUART)
                    blocks.append(spec[kind, rows, :] * cc + swapped[kind, rows, :] * ss)
                moved[kind].append(split(jnp.concatenate(blocks, axis=0)))
        got = []
        for kind in range(2):
            high = jnp.concatenate([m[0] for m in moved[kind]], axis=1)
            low = jnp.concatenate([m[1] for m in moved[kind]], axis=1)
            got.append(jnp.dot(inverse[kind], cat_right((high, low)), preferred_element_type=F32))
        near, far = got[0] + got[1], got[0] - got[1]
        for i in range(2):
            back[2 * pair + i, 0:HALF] = near[:, 128 * i : 128 * i + 128]
            back[2 * pair + i, HALF:N] = far[:, 128 * i : 128 * i + 128]
    pos = pos_ref[0]
    for slot in range(8):
        p = dest_of(pos, slot)
        base = base_of(lower_ref, p)
        for j in range(NEED):
            outs[slot][j] = back[base + j, pl.ds(pl.multiple_of(64 * p, 64), 64), :]


def base_of(lower_ref, p):
    base = lower_ref[p, 0]
    for q in range(1, 8):
        base = jnp.minimum(base, lower_ref[p, q])
    return jnp.minimum(base, NREF - NEED)


def inverse_y(f, pos_ref, lower_ref, weight_ref, source_ref, even_ref, odd_ref, *refs):
    came = refs[:8]
    pieces = refs[-1]
    pos = pos_ref[0]
    for slot in range(8):
        pieces[source_of(pos, slot)] = came[slot][...]
    first = low_lanes((64, 128))
    halves = []
    for kind, ref in enumerate((even_ref, odd_ref)):
        rows = []
        for j in range(NEED):
            re, im = [], []
            for m in range(2):
                a = pieces[4 * kind + 2 * m, j]
                b = pieces[4 * kind + 2 * m + 1, j]
                re.append(jnp.where(first, a, pltpu.roll(b, 64, 1)))
                im.append(jnp.where(first, pltpu.roll(a, 64, 1), b))
            rows += [jnp.concatenate(re, axis=1), jnp.concatenate(im, axis=1)]
        halves.append(dot3(split(jnp.concatenate(rows, axis=0)), both(ref)))
    base = base_of(lower_ref, pos)
    lane = low_lanes((1, 128))
    coef = []
    for j in range(NEED):
        tiles = []
        for q in range(8):
            lower, weight = lower_ref[pos, q] - base, weight_ref[pos, q]
            tiles.append(jnp.where(lower == j, weight, 0.0) + jnp.where(lower + 1 == j, 1.0 - weight, 0.0))
        coef.append([jnp.where(lane, tiles[2 * t], tiles[2 * t + 1]) for t in range(4)])
    field = [[None] * 4, [None] * 4]
    for j in range(NEED):
        for c in range(2):
            rows = slice(128 * j + 64 * c, 128 * j + 64 * c + 64)
            for t in range(4):
                lanes = slice(128 * (t % 2), 128 * (t % 2) + 128)
                u, v = halves[0][rows, lanes], halves[1][rows, lanes]
                term = (u + v if t < 2 else u - v) * coef[j][t]
                field[c][t] = term if j == 0 else field[c][t] + term
    image = []
    for t in range(4):
        lanes = slice(128 * t, 128 * t + 128)
        image.append(field[0][t] * source_ref[f, :, 0, lanes] + field[1][t] * source_ref[f, :, 1, lanes])
    if f == 0:
        out_ref, part_ref = refs[8:10]
        for t in range(4):
            lanes = slice(128 * t, 128 * t + 128)
            part_ref[:, lanes] = image[t]
            for c in range(2):
                out_ref[c, :, lanes] = field[c][t]
        return
    other_ref, part_ref, out_ref, image_ref = refs[8:12]
    group = lax.broadcasted_iota(jnp.int32, (8, 128), 1) // 16
    for t in range(4):
        lanes = slice(128 * t, 128 * t + 128)
        total = (image[t] + part_ref[:, lanes]) * (1.0 / 8.0)
        cells = [total[8 * b : 8 * b + 8] for b in range(8)]
        for bit in (1, 2, 4):
            low = (group & bit) == 0
            new = [None] * 8
            for b in range(8):
                if b & bit:
                    continue
                x, y = cells[b], cells[b | bit]
                new[b] = jnp.where(low, x, pltpu.roll(y, 16 * bit, 1))
                new[b | bit] = jnp.where(low, pltpu.roll(x, 128 - 16 * bit, 1), y)
            cells = new
        for g in range(8):
            image_ref[8 * t + g] = cells[g]
        for c in range(2):
            out_ref[0, :, c, lanes] = other_ref[c, :, lanes]
            out_ref[1, :, c, lanes] = field[c][t]


def sum_image(came_ref, out_ref):
    total = jnp.sum(came_ref[...], axis=0)
    for b in range(8):
        out_ref[0, 8 * b : 8 * b + 8, :] = total[:, 16 * b : 16 * b + 16]


VM = pl.BlockSpec(memory_space=pltpu.VMEM)
SM = pl.BlockSpec(memory_space=pltpu.SMEM)


def call(body, out, specs, scratch=(), f=None):
    many = isinstance(out, (tuple, list))
    return pl.pallas_call(
        body if f is None else functools.partial(body, f),
        out_shape=out,
        in_specs=specs,
        out_specs=tuple(VM for _ in out) if many else VM,
        scratch_shapes=list(scratch),
        compiler_params=pltpu.CompilerParams(vmem_limit_bytes=16 * 2**20),
        interpret=INTERPRET,
    )


def shape(*dims):
    return jax.ShapeDtypeStruct(dims, F32)


def ring(slot):
    chips, core = SLOTS[slot]
    return [(2 * x + c, 2 * ((x + chips) % 4) + (c + core) % 2) for x in range(4) for c in range(2)]


def whole(wave_field, source_field, omegas, velocities, lower_ref, blend_weight):
    pos = lax.axis_index("pencil").reshape(1)
    even, odd, odd_t, ae, ao, be, bo = (jnp.asarray(t) for t in tables())
    sent = call(forward_y, shape(8, 2, 64, 128), [VM] * 3)(wave_field, even, odd)
    came = lax.all_to_all(sent.reshape(8, 128, 128), "pencil", 0, 0, tiled=True).reshape(8, 2, 64, 128)
    phase = call(
        phases, (shape(2, NREF, QUART, 128), shape(2, NREF, QUART, 128), shape(2, NREF, 2, 8, 128)), [SM] * 3
    )(pos, omegas, velocities[0])
    pieces = []
    for f in range(2):
        sent = call(
            shift_x,
            [shape(NEED, 64, 128)] * 8,
            [SM] * 2 + [VM] * 8,
            [pltpu.VMEM((2, HALF, 128), F32)] * 2 + [pltpu.VMEM((NREF, N, 128), F32)],
            f,
        )(pos, lower_ref[0], came, *phase, ae, ao, be, bo)
        got = []
        for slot in range(7):
            got.append(lax.ppermute(sent[slot], "pencil", ring(slot)))
        pieces.append(got + [sent[7]])
    scratch = [pltpu.VMEM((8, NEED, 64, 128), F32)]
    early = (pos, lower_ref[0], blend_weight[0], source_field[0], even, odd_t)
    specs = [SM] * 3 + [VM] * 11
    part = call(inverse_y, [shape(2, 64, N), shape(64, N)], specs, scratch, 0)(*early, *pieces[0])
    field, image = call(inverse_y, [shape(2, 64, 2, N), shape(32, 8, 128)], specs + [VM] * 2, scratch, 1)(
        *early, *pieces[1], *part
    )
    return finish(field, image)


def finish(field, image):
    came = lax.all_to_all(image, "freq", 0, 0, tiled=True)
    image = call(sum_image, shape(1, 64, 16), [VM])(came)
    return field, image


def solution(mesh):
    placed = (
        P("freq", "pencil", None, None),
        P(None, "freq", "pencil", None, None),
        P("freq"),
        P(),
        P(),
        P(),
    )
    return jax.shard_map(
        whole,
        mesh=mesh,
        in_specs=placed,
        out_specs=(P("freq", "pencil", None, None), P(None, "pencil", "freq")),
        check_vma=False,
    )
```

```python
import functools
import math

import jax
import jax.numpy as jnp
import numpy as np
from jax import lax
from jax.experimental import pallas as pl
from jax.experimental.pallas import tpu as pltpu
from jax.sharding import PartitionSpec as P


N = 512
NREF = 6
NEED = 3
STEP = 10.0
UNIT = 2.0 * math.pi / (N * 12.5)
HALF = N // 2
QUART = N // 4
SLOTS = ((2, 0), (2, 1), (1, 0), (1, 1), (3, 0), (3, 1), (0, 1), (0, 0))
BF = jnp.bfloat16
F32 = jnp.float32
INTERPRET = False


def split(values):
    high = values.astype(BF)
    return high, (values - high.astype(F32)).astype(BF)


def tables():
    place = np.arange(HALF)
    cas = lambda k: (lambda t: np.cos(t) + np.sin(t))((place[:, None] * k[None, :] % N) * (2.0 * np.pi / N)) / np.sqrt(N)
    even, odd = cas(2 * place), cas(2 * place + 1)
    j = np.arange(QUART)
    fold_even = cas(np.concatenate([2 * j, [HALF], N - 2 * j[1:]]))
    fold_odd = cas(np.concatenate([2 * j + 1, N - 1 - 2 * j]))
    out = []
    for table in (even, odd, odd.T, fold_even.T, fold_odd.T, fold_even, fold_odd):
        high = np.asarray(table, np.float32).astype(jnp.bfloat16)
        low = (table - high.astype(np.float64)).astype(np.float32).astype(jnp.bfloat16)
        out.append(np.stack([high, low]))
    return out


def cat_left(pair):
    high, low = pair
    return jnp.concatenate([high, high, low], axis=1)


def cat_right(pair):
    high, low = pair
    return jnp.concatenate([high, low, high], axis=0)


def dot3(left, right):
    return jnp.dot(cat_left(left), cat_right(right), preferred_element_type=F32)


def both(ref):
    return ref[0], ref[1]


def low_lanes(shape):
    return lax.broadcasted_iota(jnp.int32, shape, len(shape) - 1) < 64


def forward_y(pos_ref, wave_hbm, even_hbm, odd_hbm, *refs):
    outs, (wave_ref, even_ref, odd_ref, sem, ready) = refs[:8], refs[8:]
    pairs = ((wave_hbm, wave_ref), (even_hbm, even_ref), (odd_hbm, odd_ref))
    copies = [pltpu.make_async_copy(src, dst, sem.at[i]) for i, (src, dst) in enumerate(pairs)]
    for copy in copies:
        copy.start()
    for copy in copies:
        copy.wait()
    rows = jnp.concatenate([wave_ref[f, :, c, :] for f in range(2) for c in range(2)], axis=0)
    near, far = rows[:, :HALF], rows[:, HALF:]
    first = low_lanes((64, 128))
    for kind, (mixed, ref) in enumerate(((near + far, even_ref), (near - far, odd_ref))):
        spectrum = dot3(split(mixed), both(ref))
        for f in range(2):
            for m in range(2):
                lanes = slice(128 * m, 128 * m + 128)
                re = spectrum[128 * f : 128 * f + 64, lanes]
                im = spectrum[128 * f + 64 : 128 * f + 128, lanes]
                ready[4 * kind + 2 * m, f] = jnp.where(first, re, pltpu.roll(im, 64, 1))
                ready[4 * kind + 2 * m + 1, f] = jnp.where(first, pltpu.roll(re, 64, 1), im)
    for slot in range(8):
        outs[slot][...] = ready[dest_of(pos_ref[0], slot)]


def phase_of(q):
    root = jnp.sqrt(jnp.abs(q)) * STEP
    u = jnp.maximum(q, 0.0) * (STEP * STEP)
    cosine = jnp.full_like(u, 1.0 / math.factorial(16))
    for k in range(7, -1, -1):
        cosine = cosine * u + (-1.0) ** k / math.factorial(2 * k)
    sine = jnp.full_like(u, -1.0 / math.factorial(15))
    for k in range(6, -1, -1):
        sine = sine * u + (-1.0) ** k / math.factorial(2 * k + 1)
    damping = jnp.exp(-root)
    moving = q > 0.0
    return jnp.where(moving, cosine, damping), jnp.where(moving, sine * root, 0.0)


def phases(pos_ref, omega_ref, speed_ref, cos_ref, sin_ref, nyq_ref):
    lane = lax.broadcasted_iota(jnp.int32, (QUART, 128), 1)
    row = lax.broadcasted_iota(jnp.int32, (QUART, 128), 0)
    pos = pos_ref[0]
    ky = 2 * (64 * (pos % 4) + (lane & 63)) + pos // 4
    ky = jnp.where(ky < HALF, ky, ky - N).astype(F32) * UNIT
    kx = (2 * row + lane // 64).astype(F32) * UNIT
    ky2 = ky * ky
    radial = kx * kx + ky2
    edge = (HALF * UNIT) ** 2 + ky2[:8]
    for f in range(2):
        for r in range(NREF):
            ratio = omega_ref[f] / speed_ref[r]
            square = ratio * ratio
            c, s = phase_of(square - radial)
            cos_ref[f, r] = c
            sin_ref[f, r] = s
            c, s = phase_of(square - edge)
            nyq_ref[f, r, 0] = c
            nyq_ref[f, r, 1] = s


def dest_of(pos, slot):
    chips, core = SLOTS[slot]
    return ((pos // 2 + chips) % 4) * 2 + (pos % 2 + core) % 2


def source_of(pos, slot):
    chips, core = SLOTS[slot]
    return ((pos // 2 + 4 - chips) % 4) * 2 + (pos % 2 + core) % 2


def shift_x(f, pos_ref, lower_hbm, cos_ref, sin_ref, nyq_ref, ae_ref, ao_ref, be_ref, bo_ref, *refs):
    came, outs, (spec, swapped, back, lower_ref, sem, wave) = refs[:8], refs[8:16], refs[16:]
    fetch = pltpu.make_async_copy(lower_hbm, lower_ref, sem)
    fetch.start()
    pos = pos_ref[0]
    for slot in range(8):
        wave[source_of(pos, slot)] = came[slot][f]
    near = wave[0:4].reshape(HALF, 128)
    far = wave[4:8].reshape(HALF, 128)
    for kind, (mixed, ref) in enumerate(((near + far, ae_ref), (near - far, ao_ref))):
        found = dot3(both(ref), split(mixed))
        spec[kind] = found
        swapped[kind] = pltpu.roll(found, 64, 1)
    first = low_lanes((QUART, 128))
    first8 = low_lanes((8, 128))
    top = lax.broadcasted_iota(jnp.int32, (8, 128), 0) == 0
    inverse = (cat_left(both(be_ref)), cat_left(both(bo_ref)))
    for pair in range(NREF // 2):
        moved = [[], []]
        for r in (2 * pair, 2 * pair + 1):
            c = cos_ref[f, r]
            s = sin_ref[f, r]
            cr = pltpu.roll(c, 64, 1)
            sr = pltpu.roll(s, 64, 1)
            parts = (
                (jnp.where(first, c, cr), jnp.where(first, -s, sr)),
                (jnp.where(first, cr, c), jnp.where(first, -sr, s)),
            )
            nc = nyq_ref[f, r, 0]
            ns = nyq_ref[f, r, 1]
            ns = jnp.where(first8, -ns, ns)
            for kind in range(2):
                blocks = []
                for block in range(2):
                    cc, ss = parts[kind]
                    if kind == 0 and block == 1:
                        cc = jnp.concatenate([jnp.where(top, nc, cc[:8]), cc[8:]], axis=0)
                        ss = jnp.concatenate([jnp.where(top, ns, ss[:8]), ss[8:]], axis=0)
                    rows = pl.ds(QUART * block, QUART)
                    blocks.append(spec[kind, rows, :] * cc + swapped[kind, rows, :] * ss)
                moved[kind].append(split(jnp.concatenate(blocks, axis=0)))
        got = []
        for kind in range(2):
            high = jnp.concatenate([m[0] for m in moved[kind]], axis=1)
            low = jnp.concatenate([m[1] for m in moved[kind]], axis=1)
            got.append(jnp.dot(inverse[kind], cat_right((high, low)), preferred_element_type=F32))
        near, far = got[0] + got[1], got[0] - got[1]
        for i in range(2):
            back[2 * pair + i, 0:HALF] = near[:, 128 * i : 128 * i + 128]
            back[2 * pair + i, HALF:N] = far[:, 128 * i : 128 * i + 128]
    fetch.wait()
    for slot in range(8):
        p = dest_of(pos, slot)
        base = base_of(lower_ref, p)
        for j in range(NEED):
            outs[slot][j] = back[base + j, pl.ds(pl.multiple_of(64 * p, 64), 64), :]


def base_of(lower_ref, p):
    base = lower_ref[0, p, 0]
    for q in range(1, 8):
        base = jnp.minimum(base, lower_ref[0, p, q])
    return jnp.minimum(base, NREF - NEED)


def inverse_y(f, pos_ref, lower_hbm, weight_hbm, source_ref, even_ref, odd_ref, *refs):
    came = refs[:8]
    pieces, lower_ref, weight_ref, sem = refs[-4:]
    fetches = (
        pltpu.make_async_copy(lower_hbm, lower_ref, sem.at[0]),
        pltpu.make_async_copy(weight_hbm, weight_ref, sem.at[1]),
    )
    for fetch in fetches:
        fetch.start()
    pos = pos_ref[0]
    for slot in range(8):
        pieces[source_of(pos, slot)] = came[slot][...]
    first = low_lanes((64, 128))
    halves = []
    for kind, ref in enumerate((even_ref, odd_ref)):
        rows = []
        for j in range(NEED):
            re, im = [], []
            for m in range(2):
                a = pieces[4 * kind + 2 * m, j]
                b = pieces[4 * kind + 2 * m + 1, j]
                re.append(jnp.where(first, a, pltpu.roll(b, 64, 1)))
                im.append(jnp.where(first, pltpu.roll(a, 64, 1), b))
            rows += [jnp.concatenate(re, axis=1), jnp.concatenate(im, axis=1)]
        halves.append(dot3(split(jnp.concatenate(rows, axis=0)), both(ref)))
    for fetch in fetches:
        fetch.wait()
    base = base_of(lower_ref, pos)
    lane = low_lanes((1, 128))
    coef = []
    for j in range(NEED):
        tiles = []
        for q in range(8):
            lower, weight = lower_ref[0, pos, q] - base, weight_ref[0, pos, q]
            tiles.append(jnp.where(lower == j, weight, 0.0) + jnp.where(lower + 1 == j, 1.0 - weight, 0.0))
        coef.append([jnp.where(lane, tiles[2 * t], tiles[2 * t + 1]) for t in range(4)])
    field = [[None] * 4, [None] * 4]
    for j in range(NEED):
        for c in range(2):
            rows = slice(128 * j + 64 * c, 128 * j + 64 * c + 64)
            for t in range(4):
                lanes = slice(128 * (t % 2), 128 * (t % 2) + 128)
                u, v = halves[0][rows, lanes], halves[1][rows, lanes]
                term = (u + v if t < 2 else u - v) * coef[j][t]
                field[c][t] = term if j == 0 else field[c][t] + term
    image = []
    for t in range(4):
        lanes = slice(128 * t, 128 * t + 128)
        image.append(field[0][t] * source_ref[f, :, 0, lanes] + field[1][t] * source_ref[f, :, 1, lanes])
    out_ref, image_ref = refs[8:10] if f == 0 else refs[9:11]
    for t in range(4):
        lanes = slice(128 * t, 128 * t + 128)
        for c in range(2):
            out_ref[c, :, lanes] = field[c][t]
        if f == 0:
            image_ref[:, lanes] = image[t]
    if f == 0:
        return
    part_ref = refs[8]
    group = lax.broadcasted_iota(jnp.int32, (8, 128), 1) // 16
    for t in range(4):
        lanes = slice(128 * t, 128 * t + 128)
        total = (image[t] + part_ref[:, lanes]) * (1.0 / 8.0)
        cells = [total[8 * b : 8 * b + 8] for b in range(8)]
        for bit in (1, 2, 4):
            low = (group & bit) == 0
            new = [None] * 8
            for b in range(8):
                if b & bit:
                    continue
                x, y = cells[b], cells[b | bit]
                new[b] = jnp.where(low, x, pltpu.roll(y, 16 * bit, 1))
                new[b | bit] = jnp.where(low, pltpu.roll(x, 128 - 16 * bit, 1), y)
            cells = new
        for g in range(8):
            image_ref[8 * t + g] = cells[g]


def store_field(first_ref, second_ref, out_ref):
    for f, ref in enumerate((first_ref, second_ref)):
        for c in range(2):
            out_ref[f, :, c, :] = ref[c]


def sum_image(came_ref, out_ref):
    total = jnp.sum(came_ref[...], axis=0).T
    out_ref[0] = jnp.concatenate([total[16 * b : 16 * b + 16] for b in range(8)], axis=1)


VM = pl.BlockSpec(memory_space=pltpu.VMEM)
SM = pl.BlockSpec(memory_space=pltpu.SMEM)
HB = pl.BlockSpec(memory_space=pltpu.HBM)
TILES = (1, 8, 8)


def call(body, out, specs, scratch=(), f=None, grant=16):
    many = isinstance(out, (tuple, list))
    return pl.pallas_call(
        body if f is None else functools.partial(body, f),
        out_shape=out,
        in_specs=specs,
        out_specs=tuple(VM for _ in out) if many else VM,
        scratch_shapes=list(scratch),
        compiler_params=pltpu.CompilerParams(vmem_limit_bytes=grant * 2**20),
        interpret=INTERPRET,
    )


def shape(*dims):
    return jax.ShapeDtypeStruct(dims, F32)


def ring(slot):
    chips, core = SLOTS[slot]
    return [(2 * x + c, 2 * ((x + chips) % 4) + (c + core) % 2) for x in range(4) for c in range(2)]


def exchange(sent):
    got = []
    for slot in range(7):
        got.append(lax.ppermute(sent[slot], "pencil", ring(slot)))
    return got + [sent[7]]


def whole(wave_field, source_field, omegas, velocities, lower_ref, blend_weight):
    pos = lax.axis_index("pencil").reshape(1)
    even, odd, odd_t, ae, ao, be, bo = (jnp.asarray(t) for t in tables())
    sent = call(
        forward_y,
        [shape(2, 64, 128)] * 8,
        [SM] + [HB] * 3,
        [
            pltpu.VMEM(wave_field.shape, F32),
            pltpu.VMEM(even.shape, BF),
            pltpu.VMEM(odd.shape, BF),
            pltpu.SemaphoreType.DMA((3,)),
            pltpu.VMEM((8, 2, 64, 128), F32),
        ],
        grant=60,
    )(pos, wave_field, even, odd)
    came = exchange(sent)
    phase = call(
        phases, (shape(2, NREF, QUART, 128), shape(2, NREF, QUART, 128), shape(2, NREF, 2, 8, 128)), [SM] * 3
    )(pos, omegas, velocities[0])
    pieces = []
    for f in range(2):
        sent = call(
            shift_x,
            [shape(NEED, 64, 128)] * 8,
            [SM, HB] + [VM] * 15,
            [pltpu.VMEM((2, HALF, 128), F32)] * 2
            + [pltpu.VMEM((NREF, N, 128), F32), pltpu.SMEM(TILES, jnp.int32), pltpu.SemaphoreType.DMA]
            + [pltpu.VMEM((8, 64, 128), F32)],
            f,
        )(pos, lower_ref, *phase, ae, ao, be, bo, *came)
        pieces.append(exchange(sent))
    scratch = [
        pltpu.VMEM((8, NEED, 64, 128), F32),
        pltpu.SMEM(TILES, jnp.int32),
        pltpu.SMEM(TILES, F32),
        pltpu.SemaphoreType.DMA((2,)),
    ]
    early = (pos, lower_ref, blend_weight, source_field[0], even, odd_t)
    specs = [SM, HB, HB] + [VM] * 11
    first, part = call(inverse_y, [shape(2, 64, N), shape(64, N)], specs, scratch, 0)(*early, *pieces[0])
    second, image = call(inverse_y, [shape(2, 64, N), shape(32, 8, 128)], specs + [VM], scratch, 1)(
        *early, *pieces[1], part
    )
    return finish(first, second, image)


def finish(first, second, image):
    came = lax.all_to_all(image, "freq", 0, 0, tiled=True)
    field = call(store_field, shape(2, 64, 2, N), [VM] * 2)(first, second)
    image = call(sum_image, shape(1, 16, 64), [VM])(came)
    return field, jnp.transpose(image, (0, 2, 1))


def solution(mesh):
    placed = (
        P("freq", "pencil", None, None),
        P(None, "freq", "pencil", None, None),
        P("freq"),
        P(),
        P(),
        P(),
    )
    return jax.shard_map(
        whole,
        mesh=mesh,
        in_specs=placed,
        out_specs=(P("freq", "pencil", None, None), P(None, "pencil", "freq")),
        check_vma=False,
    )
```

```python
import functools
import math

import jax
import jax.numpy as jnp
import numpy as np
from jax import lax
from jax.experimental import pallas as pl
from jax.experimental.pallas import tpu as pltpu
from jax.sharding import PartitionSpec as P


N = 512
NREF = 6
NEED = 3
STEP = 10.0
UNIT = 2.0 * math.pi / (N * 12.5)
HALF = N // 2
QUART = N // 4
BF = jnp.bfloat16
F32 = jnp.float32
INTERPRET = False
FIRST = 60


def split(values):
    high = values.astype(BF)
    return high, (values - high.astype(F32)).astype(BF)


def tables():
    place = np.arange(HALF)
    cas = lambda k: (lambda t: np.cos(t) + np.sin(t))((place[:, None] * k[None, :] % N) * (2.0 * np.pi / N)) / np.sqrt(N)
    j = np.arange(QUART)
    fold_even = cas(np.concatenate([2 * j, [HALF], N - 2 * j[1:]]))
    fold_odd = cas(np.concatenate([2 * j + 1, N - 1 - 2 * j]))
    out = []
    for stack in ((fold_even, fold_odd), (fold_even.T, fold_odd.T)):
        table = np.stack(stack)
        high = np.asarray(table, np.float32).astype(jnp.bfloat16)
        low = (table - high.astype(np.float64)).astype(np.float32).astype(jnp.bfloat16)
        out.append(np.stack([high, low], axis=1))
    return out


def dot3(left, right):
    high = jnp.dot(jnp.concatenate(left, axis=0), right[0], preferred_element_type=F32)
    low = jnp.dot(left[0], right[1], preferred_element_type=F32)
    count = left[0].shape[0]
    return high[:count] + (high[count:] + low)


def low_lanes(shape):
    return lax.broadcasted_iota(jnp.int32, shape, len(shape) - 1) < 64


def forward_y(pos_ref, wave_hbm, table_hbm, own_ref, other_ref, wave_ref, table_ref, sem):
    pairs = ((wave_hbm, wave_ref), (table_hbm, table_ref))
    copies = [pltpu.make_async_copy(src, dst, sem.at[i]) for i, (src, dst) in enumerate(pairs)]
    for copy in copies:
        copy.start()
    for copy in copies:
        copy.wait()
    rows = jnp.concatenate([wave_ref[f, :, c, :] for f in range(2) for c in range(2)], axis=0)
    near, far = rows[:, :HALF], rows[:, HALF:]
    core = pos_ref[0] % 2
    for kind, out_ref in ((core, own_ref), (1 - core, other_ref)):
        mixed = near + far * (1 - 2 * kind).astype(F32)
        spectrum = dot3(split(mixed), (table_ref[kind, 0], table_ref[kind, 1]))
        for f in range(2):
            for c in range(2):
                start = 128 * f + 64 * c
                out_ref[f, :, HALF * c : HALF * c + HALF] = spectrum[start : start + 64]


def phase_of(q):
    root = jnp.sqrt(jnp.abs(q)) * STEP
    u = jnp.maximum(q, 0.0) * (STEP * STEP)
    cosine = jnp.full_like(u, -1.0 / math.factorial(14))
    for k in range(6, -1, -1):
        cosine = cosine * u + (-1.0) ** k / math.factorial(2 * k)
    sine = jnp.full_like(u, 1.0 / math.factorial(13))
    for k in range(5, -1, -1):
        sine = sine * u + (-1.0) ** k / math.factorial(2 * k + 1)
    damping = jnp.exp(-root)
    moving = q > 0.0
    return jnp.where(moving, cosine, damping), jnp.where(moving, sine * root, 0.0)


def rows_of(pos, i):
    return pos + i * (1 - 2 * (pos % 2))


def phases(f, pos_ref, lower_ref, omega_ref, speed_ref, cos_ref, sin_ref, nyq_ref, edge):
    lane = lax.broadcasted_iota(jnp.int32, (QUART, 128), 1)
    row = lax.broadcasted_iota(jnp.int32, (QUART, 128), 0)
    pos = pos_ref[0]
    core = pos % 2
    number = lambda values: values.astype(F32) * UNIT
    ky = number(2 * lane + core)
    ky2 = ky * ky
    bases = [base_of(lower_ref, rows_of(pos, i)) for i in range(2)]
    fix = lane == 128 * core

    def square(t):
        ratio = omega_ref[f] / speed_ref[jnp.where(t < NEED, bases[0] + t, bases[1] + t - NEED)]
        return ratio * ratio

    squares = jnp.zeros((QUART, 128), F32)
    for t in range(2 * NEED):
        squares = jnp.where(lane // 2 == t, square(t), squares)
    kx = number(2 * row + lane % 2)
    edge[0], edge[1] = phase_of(squares - (kx * kx + (HALF * UNIT) ** 2))

    def one(t, carry):
        now = square(t)
        for kind in range(2):
            kx = number(2 * row + kind)
            turn = (128 - 2 * t - kind) % 128
            for k, (ref, part) in enumerate(zip((cos_ref, sin_ref), phase_of(now - (kx * kx + ky2)))):
                ref[t, kind, :, :128] = part
                ref[t, kind, :, 128:] = jnp.where(fix, pltpu.roll(edge[k], turn, 1), part)
        for half in range(2):
            line = jnp.where(fix[:8], (HALF * UNIT) ** 2, ky2[:8]) if half else ky2[:8]
            for k, part in enumerate(phase_of(now - ((HALF * UNIT) ** 2 + line))):
                nyq_ref[t, k, :, 128 * half : 128 * half + 128] = part
        return carry

    lax.fori_loop(0, 2 * NEED, one, 0)


def shift_x(f, pos_ref, here_ref, right_ref, left_ref, far0_ref, far1_ref, cos_ref, sin_ref, nyq_ref, a_ref, b_ref, own_ref, other_ref, wave, spec):
    pos = pos_ref[0]
    chip, core = pos // 2, pos % 2
    sign = lambda flag: jnp.where(flag, 1.0, -1.0).astype(F32)
    mine = sign(chip < 2)
    theirs = sign((chip == 1) | (chip == 2))
    across = (far0_ref, far1_ref)
    for i in range(2):
        half = 64 * ((core + i) % 2)
        rows = pl.ds(pl.multiple_of(128 * (chip % 2) + half, 64), 64)
        a, b = here_ref[i], across[i][...]
        wave[0, rows, :] = a + b
        wave[1, rows, :] = (a - b) * mine
        rows = pl.ds(pl.multiple_of(128 * ((chip + 1) % 2) + half, 64), 64)
        a, b = right_ref[i], left_ref[i]
        wave[0, rows, :] = a + b
        wave[1, rows, :] = (a - b) * theirs
    for kind in range(2):
        spec[kind] = dot3((a_ref[kind, 0], a_ref[kind, 1]), split(wave[kind]))
    top = lax.broadcasted_iota(jnp.int32, (8, HALF), 0) == 0

    def one(j, carry):
        for i, out_ref in enumerate((own_ref, other_ref)):
            t = NEED * i + j
            p = rows_of(pos, i)
            rows = pl.ds(pl.multiple_of(64 * (p % 4), 64), 64)
            total = None
            for kind in range(2):
                c = cos_ref[t, kind]
                s = sin_ref[t, kind]
                pieces = []
                for block in range(2):
                    cc, ss = c, s
                    if kind == 0 and block == 1:
                        cc = jnp.concatenate([jnp.where(top, nyq_ref[t, 0], c[:8]), c[8:]], axis=0)
                        ss = jnp.concatenate([jnp.where(top, nyq_ref[t, 1], s[:8]), s[8:]], axis=0)
                    lines = slice(QUART * block, QUART * block + QUART)
                    re, im = spec[kind, lines, :HALF], spec[kind, lines, HALF:]
                    pieces.append(jnp.concatenate([re * cc - im * ss, re * ss + im * cc], axis=1))
                part = dot3((b_ref[kind, 0, rows, :], b_ref[kind, 1, rows, :]), split(jnp.concatenate(pieces, axis=0)))
                total = part if kind == 0 else total + part * sign(p < 4)
            out_ref[j] = total
        return carry

    for j in range(NEED):
        one(j, 0)


def base_of(lower_ref, p):
    base = lower_ref[p, 0]
    for q in range(1, 8):
        base = jnp.minimum(base, lower_ref[p, q])
    return jnp.minimum(base, NREF - NEED)


def inverse_y(f, pos_ref, lower_ref, weight_ref, source_ref, table_ref, own_ref, came_ref, *refs):
    pos = pos_ref[0]
    core = pos % 2
    halves = []
    for kind, ref in ((core, own_ref), (1 - core, came_ref)):
        rows = [ref[j, :, HALF * c : HALF * c + HALF] for j in range(NEED) for c in range(2)]
        halves.append(dot3(split(jnp.concatenate(rows, axis=0)), (table_ref[kind, 0], table_ref[kind, 1])))
    flip = (1 - 2 * core).astype(F32)
    base = base_of(lower_ref, pos)
    lane = low_lanes((1, 128))
    coef = []
    for j in range(NEED):
        tiles = []
        for q in range(8):
            lower, weight = lower_ref[pos, q] - base, weight_ref[pos, q]
            tiles.append(jnp.where(lower == j, weight, 0.0) + jnp.where(lower + 1 == j, 1.0 - weight, 0.0))
        row = [jnp.where(lane, tiles[2 * t], tiles[2 * t + 1]) for t in range(4)]
        coef.append(row[:2] + [row[2] * flip, row[3] * flip])
    field = [[None] * 4, [None] * 4]
    for j in range(NEED):
        for c in range(2):
            rows = slice(128 * j + 64 * c, 128 * j + 64 * c + 64)
            for t in range(4):
                lanes = slice(128 * (t % 2), 128 * (t % 2) + 128)
                u, v = halves[0][rows, lanes], halves[1][rows, lanes]
                term = (u + v if t < 2 else u - v) * coef[j][t]
                field[c][t] = term if j == 0 else field[c][t] + term
    image = []
    for t in range(4):
        lanes = slice(128 * t, 128 * t + 128)
        image.append(field[0][t] * source_ref[f, :, 0, lanes] + field[1][t] * source_ref[f, :, 1, lanes])
    out_ref, image_ref = refs[:2] if f == 0 else refs[1:3]
    for t in range(4):
        lanes = slice(128 * t, 128 * t + 128)
        for c in range(2):
            out_ref[c, :, lanes] = field[c][t]
        if f == 0:
            image_ref[:, lanes] = image[t]
    if f == 0:
        return
    part_ref = refs[0]
    group = lax.broadcasted_iota(jnp.int32, (8, 128), 1) // 16
    for t in range(4):
        lanes = slice(128 * t, 128 * t + 128)
        total = (image[t] + part_ref[:, lanes]) * (1.0 / 8.0)
        cells = [total[8 * b : 8 * b + 8] for b in range(8)]
        for bit in (1, 2, 4):
            low = (group & bit) == 0
            new = [None] * 8
            for b in range(8):
                if b & bit:
                    continue
                x, y = cells[b], cells[b | bit]
                new[b] = jnp.where(low, x, pltpu.roll(y, 16 * bit, 1))
                new[b | bit] = jnp.where(low, pltpu.roll(x, 128 - 16 * bit, 1), y)
            cells = new
        for g in range(8):
            image_ref[8 * t + g] = cells[g]


def store_field(first_ref, second_ref, out_ref):
    for f, ref in enumerate((first_ref, second_ref)):
        for c in range(2):
            out_ref[f, :, c, :] = ref[c]


def sum_image(came_ref, out_ref):
    total = jnp.sum(came_ref[...], axis=0).T
    out_ref[0] = jnp.concatenate([total[16 * b : 16 * b + 16] for b in range(8)], axis=1)


VM = pl.BlockSpec(memory_space=pltpu.VMEM)
SM = pl.BlockSpec(memory_space=pltpu.SMEM)
HB = pl.BlockSpec(memory_space=pltpu.HBM)


def call(body, out, specs, scratch=(), f=None, grant=16):
    many = isinstance(out, (tuple, list))
    return pl.pallas_call(
        body if f is None else functools.partial(body, f),
        out_shape=out,
        in_specs=specs,
        out_specs=tuple(VM for _ in out) if many else VM,
        scratch_shapes=list(scratch),
        compiler_params=pltpu.CompilerParams(vmem_limit_bytes=grant * 2**20),
        interpret=INTERPRET,
    )


def shape(*dims):
    return jax.ShapeDtypeStruct(dims, F32)


def permute(values, chips, core=0):
    pairs = [(2 * x + c, 2 * ((x + chips) % 4) + (c + core) % 2) for x in range(4) for c in range(2)]
    return lax.ppermute(values, "pencil", pairs)


def whole(wave_field, source_field, omegas, velocities, lower_ref, blend_weight):
    pos = lax.axis_index("pencil").reshape(1)
    lower, weight = lower_ref[0], blend_weight[0]
    back, ahead = (jnp.asarray(t) for t in tables())
    own, other = call(
        forward_y,
        [shape(2, 64, N)] * 2,
        [SM, HB, HB],
        [pltpu.VMEM(wave_field.shape, F32), pltpu.VMEM(back.shape, BF), pltpu.SemaphoreType.DMA((2,))],
        grant=FIRST,
    )(pos, wave_field, back)
    other = permute(other, 0, 1)
    here, right, left, far0, far1, phase = [], [], [], [], [], []
    for f in range(2):
        here.append(jnp.stack([own[f], other[f]]))
        right.append(permute(here[f], 1))
        left.append(permute(here[f], 3))
    for f in range(2):
        phase.append(
            call(
                phases,
                [shape(2 * NEED, 2, QUART, HALF)] * 2 + [shape(2 * NEED, 2, 8, HALF)],
                [SM] * 4,
                [pltpu.VMEM((2, QUART, 128), F32)],
                f=f,
            )(pos, lower, omegas, velocities[0])
        )
        far0.append(permute(right[f][0], 1))
        far1.append(permute(left[f][1], 3))
    fields, images = [], []
    for f in range(2):
        mine, theirs = call(
            shift_x,
            [shape(NEED, 64, N)] * 2,
            [SM] + [VM] * 10,
            [pltpu.VMEM((2, HALF, N), F32)] * 2,
            f,
        )(pos, here[f], right[f], left[f], far0[f], far1[f], *phase[f], ahead, back)
        came = permute(theirs, 0, 1)
        field, image = call(
            inverse_y,
            [shape(2, 64, N), shape(64, N) if f == 0 else shape(32, 8, 128)],
            [SM] * 3 + [VM] * (4 + f),
            f=f,
        )(pos, lower, weight, source_field[0], ahead, mine, came, *images)
        fields.append(field)
        images.append(image)
    return finish(*fields, images[-1])


def finish(first, second, image):
    came = lax.all_to_all(image, "freq", 0, 0, tiled=True)
    field = call(store_field, shape(2, 64, 2, N), [VM] * 2)(first, second)
    image = call(sum_image, shape(1, 16, 64), [VM])(came)
    return field, jnp.transpose(image, (0, 2, 1))


def solution(mesh):
    placed = (
        P("freq", "pencil", None, None),
        P(None, "freq", "pencil", None, None),
        P("freq"),
        P(),
        P(),
        P(),
    )
    return jax.shard_map(
        whole,
        mesh=mesh,
        in_specs=placed,
        out_specs=(P("freq", "pencil", None, None), P(None, "pencil", "freq")),
        check_vma=False,
    )
```

```python
import functools
import math

import jax
import jax.numpy as jnp
import numpy as np
from jax import lax
from jax.experimental import pallas as pl
from jax.experimental.pallas import tpu as pltpu
from jax.sharding import PartitionSpec as P


N = 512
NREF = 6
NEED = 3
STEP = 10.0
UNIT = 2.0 * math.pi / (N * 12.5)
HALF = N // 2
QUART = N // 4
BF = jnp.bfloat16
F32 = jnp.float32
INTERPRET = False
FIRST = 16


def split(values):
    high = values.astype(BF)
    return high, (values - high.astype(F32)).astype(BF)


def tables():
    place = np.arange(HALF)
    cas = lambda k: (lambda t: np.cos(t) + np.sin(t))((place[:, None] * k[None, :] % N) * (2.0 * np.pi / N)) / np.sqrt(N)
    j = np.arange(QUART)
    fold_even = cas(np.concatenate([2 * j, [HALF], N - 2 * j[1:]]))
    fold_odd = cas(np.concatenate([2 * j + 1, N - 1 - 2 * j]))
    out = []
    for stack in ((fold_even, fold_odd), (fold_even.T, fold_odd.T)):
        table = np.stack(stack)
        high = np.asarray(table, np.float32).astype(jnp.bfloat16)
        low = (table - high.astype(np.float64)).astype(np.float32).astype(jnp.bfloat16)
        out.append(np.stack([high, low], axis=1))
    return out


def dot3(left, right):
    high = jnp.dot(jnp.concatenate(left, axis=0), right[0], preferred_element_type=F32)
    low = jnp.dot(left[0], right[1], preferred_element_type=F32)
    count = left[0].shape[0]
    return high[:count] + (high[count:] + low)


def low_lanes(shape):
    return lax.broadcasted_iota(jnp.int32, shape, len(shape) - 1) < 64


def forward_y(pos_ref, wave_hbm, table_hbm, own0, own1, other0, other1, wave_ref, table_ref, sem):
    pairs = ((wave_hbm, wave_ref), (table_hbm, table_ref))
    copies = [pltpu.make_async_copy(src, dst, sem.at[i]) for i, (src, dst) in enumerate(pairs)]
    for copy in copies:
        copy.start()
    for copy in copies:
        copy.wait()
    rows = jnp.concatenate([wave_ref[f, :, c, :] for f in range(2) for c in range(2)], axis=0)
    near, far = rows[:, :HALF], rows[:, HALF:]
    core = pos_ref[0] % 2
    for kind, outs in ((core, (own0, own1)), (1 - core, (other0, other1))):
        mixed = near + far * (1 - 2 * kind).astype(F32)
        spectrum = dot3(split(mixed), (table_ref[kind, 0], table_ref[kind, 1]))
        for f in range(2):
            for c in range(2):
                start = 128 * f + 64 * c
                outs[f][:, HALF * c : HALF * c + HALF] = spectrum[start : start + 64]


def series(function, degree):
    top = (STEP * 250.0 / 1500.0) ** 2 * 1.0001
    fit = np.polynomial.chebyshev.Chebyshev.interpolate(function, degree, domain=[0.0, top])
    return [float(c) for c in fit.convert(kind=np.polynomial.Polynomial).coef]


COSINE = series(lambda u: np.cos(np.sqrt(u)), 5)
SINE = series(lambda u: np.sinc(np.sqrt(u) / np.pi), 5)


def phase_of(v):
    root = jnp.sqrt(jnp.abs(v))
    u = jnp.maximum(v, 0.0)
    cosine = COSINE[-1] * u + COSINE[-2]
    for c in COSINE[-3::-1]:
        cosine = cosine * u + c
    sine = SINE[-1] * u + SINE[-2]
    for c in SINE[-3::-1]:
        sine = sine * u + c
    moving = v > 0.0
    return jnp.where(moving, cosine, jnp.exp(-root)), jnp.where(moving, sine * root, 0.0)


def rows_of(pos, i):
    return pos + i * (1 - 2 * (pos % 2))


def phases(f, pos_ref, lower_ref, omega_ref, speed_ref, cos_ref, sin_ref, nyq_ref, edge, radial):
    lane = lax.broadcasted_iota(jnp.int32, (QUART, 128), 1)
    row = lax.broadcasted_iota(jnp.int32, (QUART, 128), 0)
    pos = pos_ref[0]
    core = pos % 2
    number = lambda values: values.astype(F32) * (UNIT * STEP)
    ky = number(2 * lane + core)
    ky2 = ky * ky
    bases = [base_of(lower_ref, rows_of(pos, i)) for i in range(2)]
    fix = lane == 128 * core

    def square(t):
        ratio = omega_ref[f] / speed_ref[jnp.where(t < NEED, bases[0] + t, bases[1] + t - NEED)]
        return ratio * ratio * (STEP * STEP)

    squares = jnp.zeros((QUART, 128), F32)
    for t in range(2 * NEED):
        squares = jnp.where(lane // 2 == t, square(t), squares)
    kx = number(2 * row + lane % 2)
    edge[0], edge[1] = phase_of(squares - (kx * kx + (HALF * UNIT * STEP) ** 2))

    for kind in range(2):
        kx = number(2 * row + kind)
        radial[kind] = kx * kx + ky2

    def one(t, carry):
        now = square(t)
        for kind in range(2):
            turn = (128 - 2 * t - kind) % 128
            for k, (ref, part) in enumerate(zip((cos_ref, sin_ref), phase_of(now - radial[kind]))):
                ref[t, kind, :, :128] = part
                ref[t, kind, :, 128:] = jnp.where(fix, pltpu.roll(edge[k], turn, 1), part)
        for half in range(2):
            line = jnp.where(fix[:8], (HALF * UNIT * STEP) ** 2, ky2[:8]) if half else ky2[:8]
            for k, part in enumerate(phase_of(now - ((HALF * UNIT * STEP) ** 2 + line))):
                nyq_ref[t, k, :, 128 * half : 128 * half + 128] = part
        return carry

    lax.fori_loop(0, 2 * NEED, one, 0, unroll=2)


def shift_x(f, pos_ref, *refs):
    cos_ref, sin_ref, nyq_ref, a_ref, b_ref, own_ref, other_ref, wave, spec = refs[-9:]
    if f == 0:
        here, right, left = ((ref.at[0], ref.at[1]) for ref in refs[:3])
    else:
        here, right, left = refs[0:2], refs[2:4], refs[4:6]
    across = refs[-11:-9]
    pos = pos_ref[0]
    chip, core = pos // 2, pos % 2
    sign = lambda flag: jnp.where(flag, 1.0, -1.0).astype(F32)
    mine = sign(chip < 2)
    theirs = sign((chip == 1) | (chip == 2))
    for i in range(2):
        half = 64 * ((core + i) % 2)
        rows = pl.ds(pl.multiple_of(128 * (chip % 2) + half, 64), 64)
        a, b = here[i][...], across[i][...]
        wave[0, rows, :] = a + b
        wave[1, rows, :] = (a - b) * mine
        rows = pl.ds(pl.multiple_of(128 * ((chip + 1) % 2) + half, 64), 64)
        a, b = right[i][...], left[i][...]
        wave[0, rows, :] = a + b
        wave[1, rows, :] = (a - b) * theirs
    for kind in range(2):
        spec[kind] = dot3((a_ref[kind, 0], a_ref[kind, 1]), split(wave[kind]))
    top = lax.broadcasted_iota(jnp.int32, (8, HALF), 0) == 0

    def one(j, carry):
        for i, out_ref in enumerate((own_ref, other_ref)):
            t = NEED * i + j
            p = rows_of(pos, i)
            rows = pl.ds(pl.multiple_of(64 * (p % 4), 64), 64)
            total = None
            for kind in range(2):
                c = cos_ref[t, kind]
                s = sin_ref[t, kind]
                pieces = []
                for block in range(2):
                    cc, ss = c, s
                    if kind == 0 and block == 1:
                        cc = jnp.concatenate([jnp.where(top, nyq_ref[t, 0], c[:8]), c[8:]], axis=0)
                        ss = jnp.concatenate([jnp.where(top, nyq_ref[t, 1], s[:8]), s[8:]], axis=0)
                    lines = slice(QUART * block, QUART * block + QUART)
                    re, im = spec[kind, lines, :HALF], spec[kind, lines, HALF:]
                    pieces.append(jnp.concatenate([re * cc - im * ss, re * ss + im * cc], axis=1))
                part = dot3((b_ref[kind, 0, rows, :], b_ref[kind, 1, rows, :]), split(jnp.concatenate(pieces, axis=0)))
                total = part if kind == 0 else total + part * sign(p < 4)
            out_ref[j] = total
        return carry

    for j in range(NEED):
        one(j, 0)


def base_of(lower_ref, p):
    base = lower_ref[p, 0]
    for q in range(1, 8):
        base = jnp.minimum(base, lower_ref[p, q])
    return jnp.minimum(base, NREF - NEED)


def inverse_y(f, pos_ref, lower_ref, weight_ref, source_ref, table_ref, own_ref, came_ref, *refs):
    pos = pos_ref[0]
    core = pos % 2
    halves = []
    for kind, ref in ((core, own_ref), (1 - core, came_ref)):
        rows = [ref[j, :, HALF * c : HALF * c + HALF] for j in range(NEED) for c in range(2)]
        halves.append(dot3(split(jnp.concatenate(rows, axis=0)), (table_ref[kind, 0], table_ref[kind, 1])))
    flip = (1 - 2 * core).astype(F32)
    base = base_of(lower_ref, pos)
    lane = low_lanes((1, 128))
    coef = []
    for j in range(NEED):
        tiles = []
        for q in range(8):
            lower, weight = lower_ref[pos, q] - base, weight_ref[pos, q]
            tiles.append(jnp.where(lower == j, weight, 0.0) + jnp.where(lower + 1 == j, 1.0 - weight, 0.0))
        row = [jnp.where(lane, tiles[2 * t], tiles[2 * t + 1]) for t in range(4)]
        coef.append(row[:2] + [row[2] * flip, row[3] * flip])
    field = [[None] * 4, [None] * 4]
    for j in range(NEED):
        for c in range(2):
            rows = slice(128 * j + 64 * c, 128 * j + 64 * c + 64)
            for t in range(4):
                lanes = slice(128 * (t % 2), 128 * (t % 2) + 128)
                u, v = halves[0][rows, lanes], halves[1][rows, lanes]
                term = (u + v if t < 2 else u - v) * coef[j][t]
                field[c][t] = term if j == 0 else field[c][t] + term
    image = []
    for t in range(4):
        lanes = slice(128 * t, 128 * t + 128)
        image.append(field[0][t] * source_ref[f, :, 0, lanes] + field[1][t] * source_ref[f, :, 1, lanes])
    out_ref, image_ref = refs[:2] if f == 0 else refs[1:3]
    for t in range(4):
        lanes = slice(128 * t, 128 * t + 128)
        for c in range(2):
            out_ref[c, :, lanes] = field[c][t]
        if f == 0:
            image_ref[:, lanes] = image[t]
    if f == 0:
        return
    part_ref = refs[0]
    group = lax.broadcasted_iota(jnp.int32, (8, 128), 1) // 16
    for t in range(4):
        lanes = slice(128 * t, 128 * t + 128)
        total = (image[t] + part_ref[:, lanes]) * (1.0 / 8.0)
        cells = [total[8 * b : 8 * b + 8] for b in range(8)]
        for bit in (1, 2, 4):
            low = (group & bit) == 0
            new = [None] * 8
            for b in range(8):
                if b & bit:
                    continue
                x, y = cells[b], cells[b | bit]
                new[b] = jnp.where(low, x, pltpu.roll(y, 16 * bit, 1))
                new[b | bit] = jnp.where(low, pltpu.roll(x, 128 - 16 * bit, 1), y)
            cells = new
        for g in range(8):
            image_ref[8 * t + g] = cells[g]


def store_field(first_ref, second_ref, out_ref):
    for f, ref in enumerate((first_ref, second_ref)):
        for c in range(2):
            out_ref[f, :, c, :] = ref[c]


def sum_image(came_ref, out_ref):
    total = jnp.sum(came_ref[...], axis=0).T
    out_ref[0] = jnp.concatenate([total[16 * b : 16 * b + 16] for b in range(8)], axis=1)


VM = pl.BlockSpec(memory_space=pltpu.VMEM)
SM = pl.BlockSpec(memory_space=pltpu.SMEM)
HB = pl.BlockSpec(memory_space=pltpu.HBM)


def call(body, out, specs, scratch=(), f=None, grant=16):
    many = isinstance(out, (tuple, list))
    return pl.pallas_call(
        body if f is None else functools.partial(body, f),
        out_shape=out,
        in_specs=specs,
        out_specs=tuple(VM for _ in out) if many else VM,
        scratch_shapes=list(scratch),
        compiler_params=pltpu.CompilerParams(vmem_limit_bytes=grant * 2**20),
        interpret=INTERPRET,
    )


def shape(*dims):
    return jax.ShapeDtypeStruct(dims, F32)


def permute(values, chips, core=0):
    pairs = [(2 * x + c, 2 * ((x + chips) % 4) + (c + core) % 2) for x in range(4) for c in range(2)]
    return lax.ppermute(values, "pencil", pairs)


def whole(wave_field, source_field, omegas, velocities, lower_ref, blend_weight):
    pos = lax.axis_index("pencil").reshape(1)
    lower, weight = lower_ref[0], blend_weight[0]
    back, ahead = (jnp.asarray(t) for t in tables())
    out = call(
        forward_y,
        [shape(64, N)] * 4,
        [SM, HB, HB],
        [pltpu.VMEM(wave_field.shape, F32), pltpu.VMEM(back.shape, BF), pltpu.SemaphoreType.DMA((2,))],
        grant=FIRST,
    )(pos, *(pltpu.with_memory_space_constraint(x, pltpu.HBM) for x in (wave_field, back)))
    blocks, phase = [], []
    for f in range(2):
        here = (out[f], permute(out[2 + f], 0, 1))
        if f == 0:
            here = jnp.stack(here)
            right = permute(here, 1)
            left = permute(here, 3)
            held = (here, right, left)
        else:
            right = [permute(here[i], 1) for i in range(2)]
            left = [permute(here[i], 3) for i in range(2)]
            held = (*here, *right, *left)
        across = (permute(right[0], 1), permute(left[1], 3))
        blocks.append((*held, *across))
        phase.append(
            call(
                phases,
                [shape(2 * NEED, 2, QUART, HALF)] * 2 + [shape(2 * NEED, 2, 8, HALF)],
                [SM] * 4,
                [pltpu.VMEM((2, QUART, 128), F32)] * 2,
                f=f,
            )(pos, lower, omegas, velocities[0])
        )
    fields, images = [], []
    for f in range(2):
        mine, theirs = call(
            shift_x,
            [shape(NEED, 64, N)] * 2,
            [SM] + [VM] * (len(blocks[f]) + 5),
            [pltpu.VMEM((2, HALF, N), F32)] * 2,
            f,
        )(pos, *blocks[f], *phase[f], ahead, back)
        came = permute(theirs, 0, 1)
        field, image = call(
            inverse_y,
            [shape(2, 64, N), shape(64, N) if f == 0 else shape(32, 8, 128)],
            [SM] * 3 + [VM] * (4 + f),
            f=f,
        )(pos, lower, weight, source_field[0], ahead, mine, came, *images)
        fields.append(field)
        images.append(image)
    return finish(*fields, images[-1])


def finish(first, second, image):
    came = lax.all_to_all(image, "freq", 0, 0, tiled=True)
    field = call(store_field, shape(2, 64, 2, N), [VM] * 2)(first, second)
    image = call(sum_image, shape(1, 16, 64), [VM])(came)
    return field, jnp.transpose(image, (0, 2, 1))


def solution(mesh):
    placed = (
        P("freq", "pencil", None, None),
        P(None, "freq", "pencil", None, None),
        P("freq"),
        P(),
        P(),
        P(),
    )
    return jax.shard_map(
        whole,
        mesh=mesh,
        in_specs=placed,
        out_specs=(P("freq", "pencil", None, None), P(None, "pencil", "freq")),
        check_vma=False,
    )
```

```python
import functools
import math

import jax
import jax.numpy as jnp
import numpy as np
from jax import lax
from jax.experimental import pallas as pl
from jax.experimental.pallas import tpu as pltpu
from jax.sharding import PartitionSpec as P


N = 512
NREF = 6
NEED = 3
STEP = 10.0
UNIT = 2.0 * math.pi / (N * 12.5)
HALF = N // 2
QUART = N // 4
BF = jnp.bfloat16
F32 = jnp.float32
INTERPRET = False
FIRST = 16


def split(values):
    high = values.astype(BF)
    return high, (values - high.astype(F32)).astype(BF)


def tables():
    place = np.arange(HALF)
    cas = lambda k: (lambda t: np.cos(t) + np.sin(t))((place[:, None] * k[None, :] % N) * (2.0 * np.pi / N)) / np.sqrt(N)
    j = np.arange(QUART)
    fold_even = cas(np.concatenate([2 * j, [HALF], N - 2 * j[1:]]))
    fold_odd = cas(np.concatenate([2 * j + 1, N - 1 - 2 * j]))
    out = []
    for stack in ((fold_even, fold_odd), (fold_even.T, fold_odd.T)):
        table = np.stack(stack)
        high = np.asarray(table, np.float32).astype(jnp.bfloat16)
        low = (table - high.astype(np.float64)).astype(np.float32).astype(jnp.bfloat16)
        out.append(np.stack([high, low], axis=1))
    return out


def dot3(left, right):
    high = jnp.dot(jnp.concatenate(left, axis=0), right[0], preferred_element_type=F32)
    low = jnp.dot(left[0], right[1], preferred_element_type=F32)
    count = left[0].shape[0]
    return high[:count] + (high[count:] + low)


def low_lanes(shape):
    return lax.broadcasted_iota(jnp.int32, shape, len(shape) - 1) < 64


def forward_y(pos_ref, wave_hbm, table_hbm, own0, own1, other0, other1, wave_ref, table_ref, sem):
    pairs = ((wave_hbm, wave_ref), (table_hbm, table_ref))
    copies = [pltpu.make_async_copy(src, dst, sem.at[i]) for i, (src, dst) in enumerate(pairs)]
    for copy in copies:
        copy.start()
    for copy in copies:
        copy.wait()
    rows = jnp.concatenate([wave_ref[f, :, c, :] for f in range(2) for c in range(2)], axis=0)
    near, far = rows[:, :HALF], rows[:, HALF:]
    core = pos_ref[0] % 2
    for kind, outs in ((core, (own0, own1)), (1 - core, (other0, other1))):
        mixed = near + far * (1 - 2 * kind).astype(F32)
        spectrum = dot3(split(mixed), (table_ref[kind, 0], table_ref[kind, 1]))
        for f in range(2):
            for c in range(2):
                start = 128 * f + 64 * c
                outs[f][:, HALF * c : HALF * c + HALF] = spectrum[start : start + 64]


def series(function, degree):
    top = (STEP * 250.0 / 1500.0) ** 2 * 1.0001
    fit = np.polynomial.chebyshev.Chebyshev.interpolate(function, degree, domain=[0.0, top])
    return [float(c) for c in fit.convert(kind=np.polynomial.Polynomial).coef]


COSINE = series(lambda u: np.cos(np.sqrt(u)), 5)
SINE = series(lambda u: np.sinc(np.sqrt(u) / np.pi), 5)


def phase_of(v):
    root = jnp.sqrt(jnp.abs(v))
    u = jnp.maximum(v, 0.0)
    cosine = COSINE[-1] * u + COSINE[-2]
    for c in COSINE[-3::-1]:
        cosine = cosine * u + c
    sine = SINE[-1] * u + SINE[-2]
    for c in SINE[-3::-1]:
        sine = sine * u + c
    moving = v > 0.0
    return jnp.where(moving, cosine, jnp.exp(-root)), jnp.where(moving, sine * root, 0.0)


def rows_of(pos, i):
    return pos + i * (1 - 2 * (pos % 2))


def phases(f, pos_ref, lower_ref, omega_ref, speed_ref, cos_ref, sin_ref, nyq_ref, edge, radial):
    lane = lax.broadcasted_iota(jnp.int32, (QUART, 128), 1)
    row = lax.broadcasted_iota(jnp.int32, (QUART, 128), 0)
    pos = pos_ref[0]
    core = pos % 2
    number = lambda values: values.astype(F32) * (UNIT * STEP)
    ky = number(2 * lane + core)
    ky2 = ky * ky
    bases = [base_of(lower_ref, rows_of(pos, i)) for i in range(2)]
    fix = lane == 128 * core

    def square(t):
        ratio = omega_ref[f] / speed_ref[jnp.where(t < NEED, bases[0] + t, bases[1] + t - NEED)]
        return ratio * ratio * (STEP * STEP)

    squares = jnp.zeros((QUART, 128), F32)
    for t in range(2 * NEED):
        squares = jnp.where(lane // 2 == t, square(t), squares)
    kx = number(2 * row + lane % 2)
    edge[0], edge[1] = phase_of(squares - (kx * kx + (HALF * UNIT * STEP) ** 2))

    for kind in range(2):
        kx = number(2 * row + kind)
        radial[kind] = kx * kx + ky2

    def one(t, carry):
        now = square(t)
        for kind in range(2):
            turn = (128 - 2 * t - kind) % 128
            for k, (ref, part) in enumerate(zip((cos_ref, sin_ref), phase_of(now - radial[kind]))):
                ref[t, kind, :, :128] = part
                ref[t, kind, :, 128:] = jnp.where(fix, pltpu.roll(edge[k], turn, 1), part)
        for half in range(2):
            line = jnp.where(fix[:8], (HALF * UNIT * STEP) ** 2, ky2[:8]) if half else ky2[:8]
            for k, part in enumerate(phase_of(now - ((HALF * UNIT * STEP) ** 2 + line))):
                nyq_ref[t, k, :, 128 * half : 128 * half + 128] = part
        return carry

    lax.fori_loop(0, 2 * NEED, one, 0, unroll=2)


def shift_x(f, pos_ref, *refs):
    cos_ref, sin_ref, nyq_ref, a_ref, b_ref, own_ref, other_ref, wave, spec = refs[-9:]
    if f == 0:
        here, right, left = ((ref.at[0], ref.at[1]) for ref in refs[:3])
    else:
        here, right, left = refs[0:2], refs[2:4], refs[4:6]
    across = refs[-11:-9]
    pos = pos_ref[0]
    chip, core = pos // 2, pos % 2
    sign = lambda flag: jnp.where(flag, 1.0, -1.0).astype(F32)
    mine = sign(chip < 2)
    theirs = sign((chip == 1) | (chip == 2))
    for i in range(2):
        half = 64 * ((core + i) % 2)
        rows = pl.ds(pl.multiple_of(128 * (chip % 2) + half, 64), 64)
        a, b = here[i][...], across[i][...]
        wave[0, rows, :] = a + b
        wave[1, rows, :] = (a - b) * mine
        rows = pl.ds(pl.multiple_of(128 * ((chip + 1) % 2) + half, 64), 64)
        a, b = right[i][...], left[i][...]
        wave[0, rows, :] = a + b
        wave[1, rows, :] = (a - b) * theirs
    for kind in range(2):
        spec[kind] = dot3((a_ref[kind, 0], a_ref[kind, 1]), split(wave[kind]))
    top = lax.broadcasted_iota(jnp.int32, (8, HALF), 0) == 0

    def one(j, carry):
        for i, out_ref in enumerate((own_ref, other_ref)):
            t = NEED * i + j
            p = rows_of(pos, i)
            rows = pl.ds(pl.multiple_of(64 * (p % 4), 64), 64)
            total = None
            for kind in range(2):
                c = cos_ref[t, kind]
                s = sin_ref[t, kind]
                pieces = []
                for block in range(2):
                    cc, ss = c, s
                    if kind == 0 and block == 1:
                        cc = jnp.concatenate([jnp.where(top, nyq_ref[t, 0], c[:8]), c[8:]], axis=0)
                        ss = jnp.concatenate([jnp.where(top, nyq_ref[t, 1], s[:8]), s[8:]], axis=0)
                    lines = slice(QUART * block, QUART * block + QUART)
                    re, im = spec[kind, lines, :HALF], spec[kind, lines, HALF:]
                    pieces.append(jnp.concatenate([re * cc - im * ss, re * ss + im * cc], axis=1))
                part = dot3((b_ref[kind, 0, rows, :], b_ref[kind, 1, rows, :]), split(jnp.concatenate(pieces, axis=0)))
                total = part if kind == 0 else total + part * sign(p < 4)
            out_ref[j] = total
        return carry

    for j in range(NEED):
        one(j, 0)


def base_of(lower_ref, p):
    base = lower_ref[p, 0]
    for q in range(1, 8):
        base = jnp.minimum(base, lower_ref[p, q])
    return jnp.minimum(base, NREF - NEED)


def inverse_y(f, pos_ref, lower_ref, weight_ref, source_ref, table_ref, own_ref, came_ref, *refs):
    pos = pos_ref[0]
    core = pos % 2
    halves = []
    for kind, ref in ((core, own_ref), (1 - core, came_ref)):
        rows = [ref[j, :, HALF * c : HALF * c + HALF] for j in range(NEED) for c in range(2)]
        halves.append(dot3(split(jnp.concatenate(rows, axis=0)), (table_ref[kind, 0], table_ref[kind, 1])))
    flip = (1 - 2 * core).astype(F32)
    base = base_of(lower_ref, pos)
    lane = low_lanes((1, 128))
    coef = []
    for j in range(NEED):
        tiles = []
        for q in range(8):
            lower, weight = lower_ref[pos, q] - base, weight_ref[pos, q]
            tiles.append(jnp.where(lower == j, weight, 0.0) + jnp.where(lower + 1 == j, 1.0 - weight, 0.0))
        row = [jnp.where(lane, tiles[2 * t], tiles[2 * t + 1]) for t in range(4)]
        coef.append(row[:2] + [row[2] * flip, row[3] * flip])
    field = [[None] * 4, [None] * 4]
    for j in range(NEED):
        for c in range(2):
            rows = slice(128 * j + 64 * c, 128 * j + 64 * c + 64)
            for t in range(4):
                lanes = slice(128 * (t % 2), 128 * (t % 2) + 128)
                u, v = halves[0][rows, lanes], halves[1][rows, lanes]
                term = (u + v if t < 2 else u - v) * coef[j][t]
                field[c][t] = term if j == 0 else field[c][t] + term
    image = []
    for t in range(4):
        lanes = slice(128 * t, 128 * t + 128)
        image.append(field[0][t] * source_ref[f, :, 0, lanes] + field[1][t] * source_ref[f, :, 1, lanes])
    out_ref, image_ref = refs[:2] if f == 0 else refs[1:3]
    if f == 0:
        for t in range(4):
            lanes = slice(128 * t, 128 * t + 128)
            image_ref[:, lanes] = image[t]
            for c in range(2):
                out_ref[c, :, lanes] = field[c][t]
        return
    part_ref, (packed, sem) = refs[0], refs[3:]
    copies = []
    group = lax.broadcasted_iota(jnp.int32, (8, 128), 1) // 16
    for t in range(4):
        lanes = slice(128 * t, 128 * t + 128)
        total = (image[t] + part_ref[:, lanes]) * (1.0 / 8.0)
        cells = [total[8 * b : 8 * b + 8] for b in range(8)]
        for bit in (1, 2, 4):
            low = (group & bit) == 0
            new = [None] * 8
            for b in range(8):
                if b & bit:
                    continue
                x, y = cells[b], cells[b | bit]
                new[b] = jnp.where(low, x, pltpu.roll(y, 16 * bit, 1))
                new[b | bit] = jnp.where(low, pltpu.roll(x, 128 - 16 * bit, 1), y)
            cells = new
        for g in range(8):
            packed[8 * t + g] = cells[g]
        rows = pl.ds(8 * t, 8)
        copies.append(pltpu.make_async_copy(packed.at[rows], image_ref.at[rows], sem.at[t]))
        copies[t].start()
    for t in range(4):
        lanes = slice(128 * t, 128 * t + 128)
        for c in range(2):
            out_ref[c, :, lanes] = field[c][t]
    for copy in copies:
        copy.wait()


def store_field(first_ref, second_ref, out_ref):
    for f, ref in enumerate((first_ref, second_ref)):
        for c in range(2):
            out_ref[f, :, c, :] = ref[c]


def sum_image(came_ref, out_ref):
    total = jnp.sum(came_ref[...], axis=0).T
    out_ref[0] = jnp.concatenate([total[16 * b : 16 * b + 16] for b in range(8)], axis=1)


VM = pl.BlockSpec(memory_space=pltpu.VMEM)
SM = pl.BlockSpec(memory_space=pltpu.SMEM)
HB = pl.BlockSpec(memory_space=pltpu.HBM)


def call(body, out, specs, scratch=(), f=None, grant=16, outs=None):
    many = isinstance(out, (tuple, list))
    return pl.pallas_call(
        body if f is None else functools.partial(body, f),
        out_shape=out,
        in_specs=specs,
        out_specs=outs or (tuple(VM for _ in out) if many else VM),
        scratch_shapes=list(scratch),
        compiler_params=pltpu.CompilerParams(vmem_limit_bytes=grant * 2**20),
        interpret=INTERPRET,
    )


def shape(*dims):
    return jax.ShapeDtypeStruct(dims, F32)


def permute(values, chips, core=0):
    pairs = [(2 * x + c, 2 * ((x + chips) % 4) + (c + core) % 2) for x in range(4) for c in range(2)]
    return lax.ppermute(values, "pencil", pairs)


def whole(wave_field, source_field, omegas, velocities, lower_ref, blend_weight):
    pos = lax.axis_index("pencil").reshape(1)
    lower, weight = lower_ref[0], blend_weight[0]
    back, ahead = (jnp.asarray(t) for t in tables())
    out = call(
        forward_y,
        [shape(64, N)] * 4,
        [SM, HB, HB],
        [pltpu.VMEM(wave_field.shape, F32), pltpu.VMEM(back.shape, BF), pltpu.SemaphoreType.DMA((2,))],
        grant=FIRST,
    )(pos, *(pltpu.with_memory_space_constraint(x, pltpu.HBM) for x in (wave_field, back)))
    blocks, phase = [], []
    for f in range(2):
        here = (out[f], permute(out[2 + f], 0, 1))
        if f == 0:
            here = jnp.stack(here)
            right = permute(here, 1)
            left = permute(here, 3)
            held = (here, right, left)
        else:
            right = [permute(here[i], 1) for i in range(2)]
            left = [permute(here[i], 3) for i in range(2)]
            held = (*here, *right, *left)
        across = (permute(right[0], 1), permute(left[1], 3))
        blocks.append((*held, *across))
        phase.append(
            call(
                phases,
                [shape(2 * NEED, 2, QUART, HALF)] * 2 + [shape(2 * NEED, 2, 8, HALF)],
                [SM] * 4,
                [pltpu.VMEM((2, QUART, 128), F32)] * 2,
                f=f,
            )(pos, lower, omegas, velocities[0])
        )
    fields, images = [], []
    for f in range(2):
        mine, theirs = call(
            shift_x,
            [shape(NEED, 64, N)] * 2,
            [SM] + [VM] * (len(blocks[f]) + 5),
            [pltpu.VMEM((2, HALF, N), F32)] * 2,
            f,
        )(pos, *blocks[f], *phase[f], ahead, back)
        came = permute(theirs, 0, 1)
        field, image = call(
            inverse_y,
            [shape(2, 64, N), shape(64, N) if f == 0 else shape(32, 8, 128)],
            [SM] * 3 + [VM] * (4 + f),
            [pltpu.VMEM((32, 8, 128), F32), pltpu.SemaphoreType.DMA((4,))] if f else [],
            f=f,
            outs=(VM, HB) if f else None,
        )(pos, lower, weight, source_field[0], ahead, mine, came, *images)
        fields.append(field)
        images.append(image)
    return finish(*fields, images[-1])


def finish(first, second, image):
    came = lax.all_to_all(image, "freq", 0, 0, tiled=True)
    field = call(store_field, shape(2, 64, 2, N), [VM] * 2)(first, second)
    image = call(sum_image, shape(1, 16, 64), [VM])(came)
    return field, jnp.transpose(image, (0, 2, 1))


def solution(mesh):
    placed = (
        P("freq", "pencil", None, None),
        P(None, "freq", "pencil", None, None),
        P("freq"),
        P(),
        P(),
        P(),
    )
    return jax.shard_map(
        whole,
        mesh=mesh,
        in_specs=placed,
        out_specs=(P("freq", "pencil", None, None), P(None, "pencil", "freq")),
        check_vma=False,
    )
```
